768 devices in a mesh: wide: 32 (over x_lo, y, core), narrow: 24 (over z, x_hi).
Axes of the slice: x: 4 (x_hi: 2, x_lo: 2; x = x_hi * 2 + x_lo), y: 8, z: 12, core: 2. Of those that a mesh axis runs over, the one named last changes fastest.
Arguments:
- weights: bfloat16 [32, 3072, 384], P('wide'), may hold values from -0.1875 to 0.1875
- act_rows: bfloat16 [32, 24, 1, 720, 1024], P('wide', 'narrow'), may hold values from -6 to 6
- grad_rows: bfloat16 [32, 24, 1, 720, 1024], P('wide', 'narrow'), may hold values from -6 to 6
- row_owner: int32 [32, 24, 720], P('wide', 'narrow'), may hold values from 0 to 31, as said below
- row_slot: int32 [32, 24, 720], P('wide', 'narrow'), may hold values from 0 to 29, as said below
- slot_token: int32 [32, 24, 960], P('wide', 'narrow'), may hold values from -1 to 127, as said below
- moment_one: float32 [32, 3072, 384], P('wide', 'narrow'), may hold values from -4 to 4
- moment_two: float32 [32, 3072, 384], P('wide', 'narrow'), may hold values from 0.3 to 3
Outputs:
- token_grads: bfloat16 [32, 24, 128, 1024], P('wide', 'narrow')
- new_weights: bfloat16 [32, 3072, 384], P('wide', 'narrow')
- new_one: float32 [32, 3072, 384], P('wide', 'narrow')
- new_two: float32 [32, 3072, 384], P('wide', 'narrow')
The draws below stay inside these ranges and needn't reach their ends.
Inputs may be any that keep to these rules, and one draw needn't show every extreme that they name: `row_owner`: each device sends 30 rows to half of the owners and 15 rows to the other half; for every narrow index some owner receives 30 rows from every source. `row_slot`: the slots that one device uses for one owner are 0 up to the number of its rows for that owner minus 1, each once. `slot_token`: entry w * 30 + s at owner (o, n) is the owned token of the row that device (w, n) sends to o in slot s, and -1 exactly for the slots that device leaves empty.
All inputs are finite; a program needn't handle non-finite values.
Results may differ from the reference program's by a relative error of at most 0.01.
Values may be sent and summed in bfloat16 or wider, within the bound.
No kernel may reach another device: no remote copies, remote signals or barrier semaphores. Data moves between devices by JAX's collectives and lax.ppermute only.
A program may use at most 32 MiB of HBM per device.

```python
import math
import jax
import jax.numpy as jnp
from jax import lax

D = 1024
F = 384
EXP_COL = 1
ROWS_EXP = 720
TOK_DEV = 128
ROWS_DEV = 720
CAP = 30
EXPERTS = 32
N_WIDE = 32
N_NARROW = 24


def routing_tables(key):
    base_key = jax.random.fold_in(key, 4242)

    def one_source(source_index):
        source_key = jax.random.fold_in(base_key, source_index)
        narrow_index = source_index % N_NARROW
        full_owner = jax.random.randint(jax.random.fold_in(base_key, 900000 + narrow_index), (), 0, N_WIDE)
        owner_ranks = jax.random.permutation(jax.random.fold_in(source_key, 1), N_WIDE)
        star_rank = owner_ranks[full_owner]
        owner_ranks = jnp.where(owner_ranks == 0, star_rank, owner_ranks)
        owner_ranks = owner_ranks.at[full_owner].set(0)
        counts = jnp.where(owner_ranks < N_WIDE // 2, CAP, CAP // 2).astype(jnp.int32)
        run_ends = jnp.cumsum(counts)
        starts = run_ends - counts
        positions = jnp.arange(ROWS_DEV, dtype=jnp.int32)
        owner_sorted = jnp.sum((run_ends[None, :] <= positions[:, None]).astype(jnp.int32), axis=1)
        slot_sorted = positions - starts[owner_sorted]
        row_order = jax.random.permutation(jax.random.fold_in(source_key, 2), ROWS_DEV)
        tokens = jax.random.randint(jax.random.fold_in(source_key, 3), (N_WIDE, CAP), 0, TOK_DEV)
        filled = jnp.arange(CAP, dtype=jnp.int32)[None, :] < counts[:, None]
        token_table = jnp.where(filled, tokens, -1).astype(jnp.int32)
        return (owner_sorted[row_order].astype(jnp.int32), slot_sorted[row_order].astype(jnp.int32), token_table)
    owners, slot_rows, tables = jax.vmap(one_source)(jnp.arange(N_WIDE * N_NARROW, dtype=jnp.int32))
    owners = owners.reshape(N_WIDE, N_NARROW, ROWS_DEV)
    slot_rows = slot_rows.reshape(N_WIDE, N_NARROW, ROWS_DEV)
    tables = tables.reshape(N_WIDE, N_NARROW, N_WIDE, CAP).transpose(2, 1, 0, 3).reshape(N_WIDE, N_NARROW, N_WIDE * CAP)
    return (owners, slot_rows, tables)


def draw_row_owner(key, part):
    return routing_tables(key)[0]


def draw_row_slot(key, part):
    return routing_tables(key)[1]


def draw_slot_token(key, part):
    return routing_tables(key)[2]


def levels(rng, extent, split, least, top_value):
    def one(axis_at, blocks):
        steps = jax.random.uniform(jax.random.fold_in(jax.random.fold_in(rng, 6), axis_at), (blocks,), jnp.float32, least / len(split), top_value / len(split))
        return jnp.repeat(jnp.exp(steps), extent[axis_at] // blocks).reshape((-1,) + (1,) * (len(extent) - axis_at - 1))

    factor_of = one(*split[0])
    for cut in split[1:]:
        factor_of = factor_of * one(*cut)
    return factor_of


def normal_values(rng, extent, width, limit, cuts=(), held_as=jnp.bfloat16):
    array = width * jax.random.normal(rng, extent, jnp.float32)
    if cuts:
        array = array * levels(rng, extent, cuts, -0.22, 0.18)
    return jnp.clip(array, -limit, limit).astype(held_as)


def setup_inputs(seed: int = 0) -> dict:
    streams_of = jax.random.split(jax.random.key(seed), 9)
    return {
        "weights": normal_values(streams_of[0], (EXPERTS, 3 * D, F), D ** -0.5, 0.1875, ((0, 32),)),
        "act_rows": normal_values(streams_of[1], (N_WIDE, N_NARROW, EXP_COL, ROWS_EXP, D), 1.0, 6.0, ((0, 32), (1, 24))),
        "grad_rows": normal_values(streams_of[2], (N_WIDE, N_NARROW, EXP_COL, ROWS_EXP, D), 1.0, 6.0, ((0, 32), (1, 24))),
        "row_owner": draw_row_owner(jax.random.fold_in(streams_of[8], 71), 0),
        "row_slot": draw_row_slot(jax.random.fold_in(streams_of[8], 71), 0),
        "slot_token": draw_slot_token(jax.random.fold_in(streams_of[8], 71), 0),
        "moment_one": normal_values(streams_of[6], (EXPERTS, 3 * D, F), 0.5, 4.0, ((0, 32), (1, 24)), jnp.float32),
        "moment_two": jnp.clip(jnp.exp(math.log(3.0) - 2.3025851 * jax.random.uniform(streams_of[7], (EXPERTS, 3 * D, F), jnp.float32) ** levels(streams_of[7], (EXPERTS, 3 * D, F), ((0, 32), (1, 24)), -0.2, 0.2)), 0.3, 3.0),
    }


BETA_ONE = 0.9
BETA_TWO = 0.95
LEARN_RATE = 0.003
WEIGHT_DECAY = 0.1
EPSILON = 1e-08
CORR_ONE = 1.0 - 0.9 ** 10
CORR_TWO = 1.0 - 0.95 ** 10

def expert_backward(packed, inputs, upstream):
    model_width = inputs.shape[1]
    w_gate = packed[:model_width]
    w_up = packed[model_width:2 * model_width]
    w_down = packed[2 * model_width:]
    gate_value = jnp.dot(inputs, w_gate, preferred_element_type=jnp.float32)
    up_value = jnp.dot(inputs, w_up, preferred_element_type=jnp.float32)
    gate_prob = jax.nn.sigmoid(gate_value)
    active = gate_value * gate_prob
    hidden = (active * up_value).astype(jnp.bfloat16)
    d_hidden = jnp.dot(upstream, w_down, preferred_element_type=jnp.float32)
    d_up = (d_hidden * active).astype(jnp.bfloat16)
    d_gate = (d_hidden * up_value * gate_prob * (1.0 + gate_value * (1.0 - gate_prob))).astype(jnp.bfloat16)
    d_input = jnp.dot(d_gate, w_gate.T, preferred_element_type=jnp.float32) + jnp.dot(d_up, w_up.T, preferred_element_type=jnp.float32)
    grad_term = jnp.concatenate([jnp.dot(inputs.T, d_gate, preferred_element_type=jnp.float32), jnp.dot(inputs.T, d_up, preferred_element_type=jnp.float32), jnp.dot(upstream.T, hidden, preferred_element_type=jnp.float32)], 0)
    return (d_input.astype(jnp.bfloat16), grad_term)

def reference(weights, act_rows, grad_rows, row_owner, row_slot, slot_token, moment_one, moment_two):

    def column(wide_index):
        packed_all = lax.dynamic_slice_in_dim(weights, wide_index * EXP_COL, EXP_COL, 0)

        def narrow_step(grad_total, narrow_index):
            pieces = []
            for expert in range(EXP_COL):
                d_input, grad_term = expert_backward(packed_all[expert], act_rows[wide_index, narrow_index, expert], grad_rows[wide_index, narrow_index, expert])
                pieces.append(d_input)
                rounded = lax.optimization_barrier(grad_term.astype(jnp.bfloat16))
                grad_total = grad_total.at[expert].add(rounded.astype(jnp.float32))
            d_rows = jnp.concatenate(pieces, 0)
            slot_index = row_owner[wide_index, narrow_index] * CAP + row_slot[wide_index, narrow_index]
            outgoing = jnp.zeros((N_WIDE * CAP, D), jnp.bfloat16).at[slot_index].set(d_rows)
            return (grad_total, outgoing)
        return lax.scan(narrow_step, jnp.zeros((EXP_COL, 3 * D, F), jnp.float32), jnp.arange(N_NARROW, dtype=jnp.int32))
    grad_sums, outgoing = lax.map(column, jnp.arange(N_WIDE, dtype=jnp.int32))
    outgoing = outgoing.reshape(N_WIDE, N_NARROW, N_WIDE, CAP, D)
    token_ids = jnp.arange(TOK_DEV, dtype=jnp.int32)

    def owner_sum(owner_index):
        arrived = lax.dynamic_index_in_dim(outgoing, owner_index, 2, keepdims=False)
        arrived = jnp.transpose(arrived, (1, 0, 2, 3)).reshape(N_NARROW, N_WIDE * CAP, D)
        token_table = (slot_token[owner_index][:, None, :] == token_ids[None, :, None]).astype(jnp.float32)
        return jnp.einsum('ntk,nkd->ntd', token_table, arrived.astype(jnp.float32)).astype(jnp.bfloat16)
    token_grads = lax.map(owner_sum, jnp.arange(N_WIDE, dtype=jnp.int32))
    grad_scale = 1.0 / math.sqrt(ROWS_EXP * N_NARROW)
    gradient = grad_sums.reshape(EXPERTS, 3 * D, F) * grad_scale
    new_one = BETA_ONE * moment_one + (1.0 - BETA_ONE) * gradient
    new_two = BETA_TWO * moment_two + (1.0 - BETA_TWO) * gradient * gradient
    update = new_one / CORR_ONE / (jnp.sqrt(new_two / CORR_TWO) + EPSILON)
    new_weights = (weights.astype(jnp.float32) * (1.0 - LEARN_RATE * WEIGHT_DECAY) - LEARN_RATE * update).astype(jnp.bfloat16)
    return (token_grads, new_weights, new_one, new_two)
```

```python
import math

import jax
import jax.numpy as jnp
from jax import lax
from jax.experimental import pallas as pl
from jax.experimental.pallas import tpu as pltpu
from jax.sharding import PartitionSpec as P

BETA_ONE = 0.9
BETA_TWO = 0.95
LEARN_RATE = 0.003
WEIGHT_DECAY = 0.1
EPSILON = 1e-08
CORR_ONE = 1.0 - 0.9**10
CORR_TWO = 1.0 - 0.95**10

FRAME = 32
LANES = 128


def rows_kernel(x_ref, dy_ref, w_ref, place_ref, out_ref, pair_ref, hidden_ref):
    rows, width = x_ref.shape
    units = w_ref.shape[1]
    tile = rows // 3

    def backward(step, carry):
        at = pl.ds(pl.multiple_of(step * tile, 16), tile)
        x = x_ref[at, :]
        gate = jnp.dot(x, w_ref[:width, :], preferred_element_type=jnp.float32)
        up = jnp.dot(x, w_ref[width : 2 * width, :], preferred_element_type=jnp.float32)
        d_hidden = jnp.dot(dy_ref[at, :], w_ref[2 * width :, :], preferred_element_type=jnp.float32)
        prob = jax.nn.sigmoid(gate)
        active = gate * prob
        hidden_ref[at, :] = (active * up).astype(jnp.bfloat16)
        pair_ref[at, units:] = (d_hidden * active).astype(jnp.bfloat16)
        pair_ref[at, :units] = (d_hidden * up * prob * (1.0 + gate * (1.0 - prob))).astype(jnp.bfloat16)
        return carry

    lax.fori_loop(0, 3, backward, 0)
    block = 256

    def send(step, carry):
        start = pl.multiple_of(step * block, block)
        slots = lax.broadcasted_iota(jnp.int32, (block, rows), 0) + start
        chosen = (slots == place_ref[...]).astype(jnp.bfloat16)
        moved = jnp.dot(chosen, pair_ref[...], preferred_element_type=jnp.float32).astype(jnp.bfloat16)
        last = (((1,), (1,)), ((), ()))
        total = lax.dot_general(moved[:, :units], w_ref[:width, :], last, preferred_element_type=jnp.float32)
        total += lax.dot_general(
            moved[:, units:], w_ref[width : 2 * width, :], last, preferred_element_type=jnp.float32
        )
        out_ref[pl.ds(start, block), :] = total.astype(jnp.bfloat16)
        return carry

    lax.fori_loop(0, out_ref.shape[0] // block, send, 0)


def terms_kernel(x_ref, dy_ref, pair_ref, hidden_ref, out_ref):
    units = hidden_ref.shape[1]
    width = x_ref.shape[1]
    per = width // LANES
    first = (((0,), (0,)), ((), ()))
    for index, (left, right) in enumerate(
        ((pair_ref.at[:, :units], x_ref), (pair_ref.at[:, units:], x_ref), (hidden_ref, dy_ref))
    ):
        product = lax.dot_general(left[...], right[...], first, preferred_element_type=jnp.float32)
        product = product.astype(jnp.bfloat16)
        for block in range(per):
            out_ref[index * per + block] = product[:, block * LANES : (block + 1) * LANES]


def adam_kernel(scale, shard_ref, grad_ref, weights_ref, one_ref, two_ref, out_w, out_one, out_two):
    gradient = jnp.transpose(grad_ref[...]) * scale
    new_one = BETA_ONE * one_ref[0] + (1.0 - BETA_ONE) * gradient
    new_two = BETA_TWO * two_ref[0] + (1.0 - BETA_TWO) * gradient * gradient
    update = new_one / CORR_ONE / (jnp.sqrt(new_two / CORR_TWO) + EPSILON)
    kept = weights_ref[0].astype(jnp.float32) * (1.0 - LEARN_RATE * WEIGHT_DECAY)
    out_w[0] = (kept - LEARN_RATE * update).astype(jnp.bfloat16)
    out_one[0] = new_one
    out_two[0] = new_two


def ring_sum(term, wide, narrow):
    ring = term.shape[0]
    cores = lax.axis_index("wide")
    z, high = lax.axis_index("narrow") // 2, lax.axis_index("narrow") % 2
    way = 1 - 2 * (cores % 2)

    def hop(value, sign):
        pairs = []
        for w in range(wide):
            shift = sign * (1 - 2 * (w % 2))
            for n in range(narrow):
                to = ((n // 2 + shift) % ring) * 2 + n % 2
                pairs.append((w * narrow + n, w * narrow + to))
        return lax.ppermute(value, ("wide", "narrow"), pairs)

    def own(offset):
        at = (z + offset * way + 2 * ring) % ring
        return lax.dynamic_index_in_dim(term, at, 0, keepdims=False).astype(jnp.float32)

    far = ring // 2
    ahead, behind = own(far).astype(jnp.bfloat16), own(1 - far).astype(jnp.bfloat16)
    for step in range(1, far + 1):
        ahead = hop(ahead, 1)
        if step < far:
            behind = hop(behind, -1)
            ahead = (ahead.astype(jnp.float32) + own(far - step)).astype(jnp.bfloat16)
        if step < far - 1:
            behind = (behind.astype(jnp.float32) + own(step + 1 - far)).astype(jnp.bfloat16)
    total = ahead.astype(jnp.float32) + behind.astype(jnp.float32) + own(0)
    mine = lax.dynamic_index_in_dim(total, high, 0, keepdims=False)
    theirs = lax.dynamic_index_in_dim(total, 1 - high, 0, keepdims=False).astype(jnp.bfloat16)
    swap = [(n, n + 1 - 2 * (n % 2)) for n in range(narrow)]
    return mine + lax.ppermute(theirs, "narrow", swap).astype(jnp.float32)


def shards(weights, act_rows, grad_rows, row_owner, row_slot, slot_token, moment_one, moment_two):
    wide, narrow = lax.axis_size("wide"), lax.axis_size("narrow")
    rows, width = act_rows.shape[3:]
    units = weights.shape[2]
    shard_rows = moment_one.shape[1]
    tokens = 128
    capacity = slot_token.shape[2] // wide
    grad_scale = 1.0 / math.sqrt(rows * narrow)
    x, dy, packed = act_rows[0, 0, 0], grad_rows[0, 0, 0], weights[0]
    vmem = pl.BlockSpec(memory_space=pltpu.VMEM)

    place = row_owner[0] * FRAME + row_slot[0]
    outgoing, pair, hidden = pl.pallas_call(
        rows_kernel,
        out_shape=(
            jax.ShapeDtypeStruct((wide * FRAME, width), jnp.bfloat16),
            jax.ShapeDtypeStruct((rows, 2 * units), jnp.bfloat16),
            jax.ShapeDtypeStruct((rows, units), jnp.bfloat16),
        ),
        in_specs=[vmem] * 4,
        out_specs=(vmem,) * 3,
        cost_estimate=pl.CostEstimate(flops=5 * 10**9, bytes_accessed=9 * 10**6, transcendentals=3 * 10**5),
        name="rows",
    )(x, dy, packed, place)
    arrived = lax.all_to_all(
        outgoing.reshape(wide, FRAME, width), "wide", split_axis=0, concat_axis=0, tiled=True
    ).reshape(wide * FRAME, width)

    term = pl.pallas_call(
        terms_kernel,
        out_shape=jax.ShapeDtypeStruct((narrow, units, shard_rows), jnp.bfloat16),
        in_specs=[vmem] * 4,
        out_specs=vmem,
        cost_estimate=pl.CostEstimate(flops=2 * 10**9, bytes_accessed=7 * 10**6, transcendentals=0),
        name="terms",
    )(x, dy, pair, hidden)
    summed = ring_sum(term.reshape(narrow // 2, 2, units, shard_rows), wide, narrow)

    shard = lax.axis_index("narrow").astype(jnp.int32).reshape(1)
    block = (1, shard_rows, units)
    whole = pl.BlockSpec(block, lambda i, s: (0, 0, 0))
    new_weights, new_one, new_two = pl.pallas_call(
        lambda *refs: adam_kernel(grad_scale, *refs),
        out_shape=(
            jax.ShapeDtypeStruct(block, jnp.bfloat16),
            jax.ShapeDtypeStruct(block, jnp.float32),
            jax.ShapeDtypeStruct(block, jnp.float32),
        ),
        grid_spec=pltpu.PrefetchScalarGridSpec(
            num_scalar_prefetch=1,
            grid=(1,),
            in_specs=[
                pl.BlockSpec((units, shard_rows), lambda i, s: (0, 0)),
                pl.BlockSpec(block, lambda i, s: (0, s[0], 0)),
                whole,
                whole,
            ],
            out_specs=(whole, whole, whole),
        ),
        name="adam",
    )(shard, summed, weights, moment_one, moment_two)

    slots = jnp.pad(slot_token[0, 0].reshape(wide, capacity), ((0, 0), (0, FRAME - capacity)), constant_values=-1)
    token_ids = lax.broadcasted_iota(jnp.int32, (tokens, wide * FRAME), 0)
    token_table = (slots.reshape(1, wide * FRAME) == token_ids).astype(jnp.bfloat16)
    combined = jnp.dot(token_table, arrived, preferred_element_type=jnp.float32)
    token_grads = combined.astype(jnp.bfloat16)[None, None]
    return (token_grads, new_weights, new_one, new_two)


def solution(mesh):
    in_specs = (
        P("wide", None, None),
        P("wide", "narrow", None, None, None),
        P("wide", "narrow", None, None, None),
        P("wide", "narrow", None),
        P("wide", "narrow", None),
        P("wide", "narrow", None),
        P("wide", "narrow", None),
        P("wide", "narrow", None),
    )
    out_specs = (
        P("wide", "narrow", None, None),
        P("wide", "narrow", None),
        P("wide", "narrow", None),
        P("wide", "narrow", None),
    )
    return jax.shard_map(shards, mesh=mesh, in_specs=in_specs, out_specs=out_specs, check_vma=False)
```

```python
import math

import jax
import jax.numpy as jnp
from jax import lax
from jax.experimental import pallas as pl
from jax.experimental.pallas import tpu as pltpu
from jax.sharding import PartitionSpec as P

BETA_ONE = 0.9
BETA_TWO = 0.95
LEARN_RATE = 0.003
WEIGHT_DECAY = 0.1
EPSILON = 1e-08
CORR_ONE = 1.0 - 0.9**10
CORR_TWO = 1.0 - 0.95**10

FRAME = 32
LANES = 128

AHEAD, BEHIND, FAR, KEPT = (5, 3, 1), (-5, -3, -1), (6,), (4, -4, 2, -2, 0)
GROUPS = (AHEAD, BEHIND, FAR, *((offset,) for offset in KEPT))


def expert_kernel(narrow_ref, wide_ref, owner_ref, slot_ref, x_hbm, dy_hbm, w_hbm, *refs):
    targets, out_hbm = refs[: len(GROUPS)], refs[len(GROUPS)]
    x, dy, w, pair, hidden, terms, turned, out, in_sem, out_sem = refs[len(GROUPS) + 1 :]
    width, units = x.shape[1], w.shape[1]
    loads = [
        pltpu.make_async_copy(x_hbm, x, in_sem.at[0]),
        pltpu.make_async_copy(w_hbm.at[pl.ds(0, width)], w.at[pl.ds(0, width)], in_sem.at[1]),
        pltpu.make_async_copy(w_hbm.at[pl.ds(width, width)], w.at[pl.ds(width, width)], in_sem.at[2]),
        pltpu.make_async_copy(dy_hbm, dy, in_sem.at[3]),
        pltpu.make_async_copy(w_hbm.at[pl.ds(2 * width, width)], w.at[pl.ds(2 * width, width)], in_sem.at[4]),
    ]
    for load in loads:
        load.start()
    loads[0].wait()
    loads[1].wait()
    gate = jnp.dot(x[...], w[:width, :], preferred_element_type=jnp.float32)
    loads[2].wait()
    up = jnp.dot(x[...], w[width : 2 * width, :], preferred_element_type=jnp.float32)
    loads[3].wait()
    loads[4].wait()
    d_hidden = jnp.dot(dy[...], w[2 * width :, :], preferred_element_type=jnp.float32)
    prob = jax.nn.sigmoid(gate)
    active = gate * prob
    hidden[...] = (active * up).astype(jnp.bfloat16)
    pair[:, units:] = (d_hidden * active).astype(jnp.bfloat16)
    pair[:, :units] = (d_hidden * up * prob * (1.0 + gate * (1.0 - prob))).astype(jnp.bfloat16)
    sends = []

    ring = terms.shape[0]
    per = width // LANES
    first = (((0,), (0,)), ((), ()))
    for index, (left, right) in enumerate(((pair.at[:, :units], x), (pair.at[:, units:], x), (hidden, dy))):
        product = lax.dot_general(left[...], right[...], first, preferred_element_type=jnp.float32)
        product = product.astype(jnp.bfloat16)
        for block in range(per):
            at = index * per + block
            terms[at // 2, at % 2] = product[:, block * LANES : (block + 1) * LANES]

    z, high = narrow_ref[0] // 2, narrow_ref[0] % 2
    way = 1 - 2 * (wide_ref[0] % 2)
    for target, offsets in zip(targets, GROUPS):
        for index, offset in enumerate(offsets):
            chip = (z + offset * way + 2 * ring) % ring
            for half, which in enumerate((high, 1 - high)):
                send = pltpu.make_async_copy(terms.at[chip, which], target.at[index, half], out_sem.at[len(sends)])
                send.start()
                sends.append(send)

    place = owner_ref[...] * FRAME + slot_ref[...]
    chosen = (lax.broadcasted_iota(jnp.int32, (out.shape[0], x.shape[0]), 0) == place).astype(jnp.bfloat16)
    turned[:units, :] = jnp.transpose(w[:width, :])
    turned[units:, :] = jnp.transpose(w[width : 2 * width, :])
    moved = jnp.dot(chosen, pair[...], preferred_element_type=jnp.float32).astype(jnp.bfloat16)
    parts = 2
    block = out.shape[0] // parts
    for part in range(parts):
        at = pl.ds(part * block, block)
        total = jnp.dot(moved[part * block : (part + 1) * block], turned[...], preferred_element_type=jnp.float32)
        out[at, :] = total.astype(jnp.bfloat16)
        send = pltpu.make_async_copy(out.at[at], out_hbm.at[at], out_sem.at[len(sends)])
        send.start()
        sends.append(send)
    for send in sends:
        send.wait()


def table_kernel(slots_ref, out_ref):
    tokens, frames = out_ref.shape
    slots = slots_ref.shape[1]
    capacity = slots * FRAME // frames
    held = (lax.broadcasted_iota(jnp.int32, (tokens, slots), 0) == slots_ref[...]).astype(jnp.bfloat16)
    place = lax.broadcasted_iota(jnp.int32, (slots, frames), 1)
    within = lax.bitwise_and(place, FRAME - 1)
    source = lax.shift_right_logical(place, FRAME.bit_length() - 1) * capacity + within
    spread = (lax.broadcasted_iota(jnp.int32, (slots, frames), 0) == source) & (within < capacity)
    out_ref[...] = jnp.dot(held, spread.astype(jnp.bfloat16), preferred_element_type=jnp.float32).astype(jnp.bfloat16)


def combine_kernel(table_hbm, rows_hbm, out_ref, table, rows, sem):
    count = sem.shape[0] - 1
    block = rows.shape[0] // count
    first = pltpu.make_async_copy(table_hbm, table, sem.at[count])
    first.start()
    loads = []
    for index in range(count):
        at = pl.ds(index * block, block)
        loads.append(pltpu.make_async_copy(rows_hbm.at[at], rows.at[at], sem.at[index]))
        loads[-1].start()
    first.wait()
    total = jnp.zeros(out_ref.shape, jnp.float32)
    for index, load in enumerate(loads):
        load.wait()
        at = slice(index * block, (index + 1) * block)
        total += jnp.dot(table[:, at], rows[at, :], preferred_element_type=jnp.float32)
    out_ref[...] = total.astype(jnp.bfloat16)


def adam_kernel(scale, parts, shard_ref, *refs):
    weights_ref, one_ref, two_ref, out_w, out_one, out_two = refs[parts:]
    total = refs[0][...].astype(jnp.float32)
    for ref in refs[1:parts]:
        total += ref[...].astype(jnp.float32)
    gradient = jnp.transpose(total) * scale
    new_one = BETA_ONE * one_ref[0] + (1.0 - BETA_ONE) * gradient
    new_two = BETA_TWO * two_ref[0] + (1.0 - BETA_TWO) * gradient * gradient
    update = new_one / CORR_ONE / (jnp.sqrt(new_two / CORR_TWO) + EPSILON)
    kept = weights_ref[0].astype(jnp.float32) * (1.0 - LEARN_RATE * WEIGHT_DECAY)
    out_w[0] = (kept - LEARN_RATE * update).astype(jnp.bfloat16)
    out_one[0] = new_one
    out_two[0] = new_two


def ring_sum(ahead, behind, far, up_own, down_own, up_next, down_next, own, wide, narrow):
    ring = narrow // 2

    def hop(value, steps, flip=0):
        pairs = []
        for w in range(wide):
            shift = steps * (1 - 2 * (w % 2))
            for n in range(narrow):
                to = ((n // 2 + shift) % ring) * 2 + (n % 2 + flip) % 2
                pairs.append((w * narrow + n, w * narrow + to))
        return lax.ppermute(value, ("wide", "narrow"), pairs)

    def add(*values):
        total = values[0].astype(jnp.float32)
        for value in values[1:]:
            total += value.astype(jnp.float32)
        return total.astype(jnp.bfloat16)

    ahead = hop(ahead, 1)
    behind = hop(behind, -1)
    far = hop(far, 2)
    up = hop(add(far[0], ahead[0], up_own[0]), 2)
    down = hop(add(behind[0], down_own[0]), -2)
    up = hop(add(up, ahead[1], up_next[0]), 2)
    down = hop(add(down, behind[1], down_next[0]), -2)
    across = hop(add(up[1], down[1], ahead[2, 1], behind[2, 1], own[0, 1]), 0, 1)
    return (ahead, behind, own, up[None], down[None]), (across,)


def step(weights, act_rows, grad_rows, row_owner, row_slot, slot_token, moment_one, moment_two):
    wide, narrow = lax.axis_size("wide"), lax.axis_size("narrow")
    rows, width = act_rows.shape[3:]
    units = weights.shape[2]
    shard_rows = moment_one.shape[1]
    tokens = 128
    grad_scale = 1.0 / math.sqrt(rows * narrow)
    x, dy, packed = act_rows[0, 0, 0], grad_rows[0, 0, 0], weights[0]
    anywhere, vmem, smem = (pl.BlockSpec(memory_space=m) for m in (pl.ANY, pltpu.VMEM, pltpu.SMEM))
    half = jnp.bfloat16
    shard = lax.axis_index("narrow").astype(jnp.int32).reshape(1)
    column = lax.axis_index("wide").astype(jnp.int32).reshape(1)

    sizes = [len(group) for group in GROUPS]
    *blocks, outgoing = pl.pallas_call(
        expert_kernel,
        out_shape=tuple(jax.ShapeDtypeStruct((n, 2, units, shard_rows), half) for n in sizes)
        + (jax.ShapeDtypeStruct((wide * FRAME, width), half),),
        in_specs=[smem] * 2 + [vmem] * 2 + [anywhere] * 3,
        out_specs=(anywhere,) * (len(sizes) + 1),
        scratch_shapes=[
            pltpu.VMEM((rows, width), half),
            pltpu.VMEM((rows, width), half),
            pltpu.VMEM((3 * width, units), half),
            pltpu.VMEM((rows, 2 * units), half),
            pltpu.VMEM((rows, units), half),
            pltpu.VMEM((narrow // 2, 2, units, shard_rows), half),
            pltpu.VMEM((2 * units, width), half),
            pltpu.VMEM((wide * FRAME, width), half),
            pltpu.SemaphoreType.DMA((5,)),
            pltpu.SemaphoreType.DMA((2 * sum(sizes) + 2,)),
        ],
        cost_estimate=pl.CostEstimate(flops=7 * 10**9, bytes_accessed=12 * 10**6, transcendentals=3 * 10**5),
        name="expert",
    )(shard, column, row_owner[0], row_slot[0], x, dy, packed)
    stacks, parts = ring_sum(*blocks, wide, narrow)
    arrived = lax.all_to_all(
        outgoing.reshape(wide, FRAME, width), "wide", split_axis=0, concat_axis=0, tiled=True
    ).reshape(wide * FRAME, width)

    block = (1, shard_rows, units)
    whole = pl.BlockSpec(block, lambda i, s: (0, 0, 0))
    part = pl.BlockSpec((units, shard_rows), lambda i, s: (0, 0))
    stack = [pl.BlockSpec((None, None, units, shard_rows), lambda i, s, n=a.shape[0]: (n - 1, 0, 0, 0)) for a in stacks]
    new_weights, new_one, new_two = pl.pallas_call(
        lambda *refs: adam_kernel(grad_scale, len(stacks) + len(parts), *refs),
        out_shape=(
            jax.ShapeDtypeStruct(block, half),
            jax.ShapeDtypeStruct(block, jnp.float32),
            jax.ShapeDtypeStruct(block, jnp.float32),
        ),
        grid_spec=pltpu.PrefetchScalarGridSpec(
            num_scalar_prefetch=1,
            grid=(1,),
            in_specs=stack + [part] * len(parts) + [pl.BlockSpec(block, lambda i, s: (0, s[0], 0)), whole, whole],
            out_specs=(whole, whole, whole),
        ),
        compiler_params=pltpu.CompilerParams(vmem_limit_bytes=6 * 2**20),
        name="adam",
    )(shard, *stacks, *parts, weights, moment_one, moment_two)

    table = pl.pallas_call(
        table_kernel,
        out_shape=jax.ShapeDtypeStruct((tokens, wide * FRAME), half),
        in_specs=[vmem],
        out_specs=vmem,
        cost_estimate=pl.CostEstimate(flops=3 * 10**8, bytes_accessed=3 * 10**5, transcendentals=0),
        name="table",
    )(slot_token[0])
    combined = pl.pallas_call(
        combine_kernel,
        out_shape=jax.ShapeDtypeStruct((tokens, width), half),
        in_specs=[anywhere] * 2,
        out_specs=vmem,
        scratch_shapes=[
            pltpu.VMEM((tokens, wide * FRAME), half),
            pltpu.VMEM((wide * FRAME, width), half),
            pltpu.SemaphoreType.DMA((5,)),
        ],
        cost_estimate=pl.CostEstimate(flops=3 * 10**8, bytes_accessed=3 * 10**6, transcendentals=0),
        name="combine",
    )(table, arrived)
    return (combined[None, None], new_weights, new_one, new_two)


def solution(mesh):
    in_specs = (
        P("wide", None, None),
        P("wide", "narrow", None, None, None),
        P("wide", "narrow", None, None, None),
        P("wide", "narrow", None),
        P("wide", "narrow", None),
        P("wide", "narrow", None),
        P("wide", "narrow", None),
        P("wide", "narrow", None),
    )
    out_specs = (
        P("wide", "narrow", None, None),
        P("wide", "narrow", None),
        P("wide", "narrow", None),
        P("wide", "narrow", None),
    )
    return jax.shard_map(step, mesh=mesh, in_specs=in_specs, out_specs=out_specs, check_vma=False)
```

```python
import math

import jax
import jax.numpy as jnp
from jax import lax
from jax.experimental import pallas as pl
from jax.experimental.pallas import tpu as pltpu
from jax.sharding import PartitionSpec as P

BETA_ONE = 0.9
BETA_TWO = 0.95
LEARN_RATE = 0.003
WEIGHT_DECAY = 0.1
EPSILON = 1e-08
CORR_ONE = 1.0 - 0.9**10
CORR_TWO = 1.0 - 0.95**10

FRAME = 32
LANES = 128

AHEAD, BEHIND, FAR, KEPT = (5, 3, 1), (-5, -3, -1), (6,), (4, -4, 2, -2, 0)
GROUPS = (AHEAD, BEHIND, FAR, *((offset,) for offset in KEPT))


def expert_kernel(narrow_ref, wide_ref, owner_ref, slot_ref, x_hbm, dy_hbm, w_hbm, *refs):
    targets, out_hbm = refs[: len(GROUPS)], refs[len(GROUPS)]
    x, dy, w, w_down, pair, hidden, terms, turned, out, in_sem, out_sem = refs[len(GROUPS) + 1 :]
    width, units = x.shape[1], hidden.shape[1]
    loads = [
        pltpu.make_async_copy(x_hbm, x, in_sem.at[0]),
        pltpu.make_async_copy(w_hbm.at[pl.ds(0, width)], w.at[:, pl.ds(0, units)], in_sem.at[1]),
        pltpu.make_async_copy(w_hbm.at[pl.ds(width, width)], w.at[:, pl.ds(units, units)], in_sem.at[2]),
        pltpu.make_async_copy(dy_hbm, dy, in_sem.at[3]),
        pltpu.make_async_copy(w_hbm.at[pl.ds(2 * width, width)], w_down, in_sem.at[4]),
    ]
    for load in loads:
        load.start()
    for load in loads[:3]:
        load.wait()
    rows = x.shape[0]
    cut = -(-rows // 32) * 16
    blocks = (slice(0, cut), slice(cut, rows))
    products = [jnp.dot(x[at, :], w[...], preferred_element_type=jnp.float32) for at in blocks]
    for load in loads[3:]:
        load.wait()
    for at, both in zip(blocks, products):
        gate, up = both[:, :units], both[:, units:]
        d_hidden = jnp.dot(dy[at, :], w_down[...], preferred_element_type=jnp.float32)
        prob = jax.nn.sigmoid(gate)
        active = gate * prob
        hidden[at, :] = (active * up).astype(jnp.bfloat16)
        pair[at, units:] = (d_hidden * active).astype(jnp.bfloat16)
        pair[at, :units] = (d_hidden * up * prob * (1.0 + gate * (1.0 - prob))).astype(jnp.bfloat16)
    sends = []

    ring = terms.shape[0]
    per = width // LANES
    first = (((0,), (0,)), ((), ()))
    for start, left, right in ((0, pair, x), (2 * per, hidden, dy)):
        product = lax.dot_general(left[...], right[...], first, preferred_element_type=jnp.float32)
        product = product.astype(jnp.bfloat16)
        for at in range(start, start + per * left.shape[1] // units):
            row, block = (at - start) // per * units, at % per * LANES
            terms[at // 2, at % 2] = product[row : row + units, block : block + LANES]

    z, high = narrow_ref[0] // 2, narrow_ref[0] % 2
    way = 1 - 2 * (wide_ref[0] % 2)
    for target, offsets in zip(targets, GROUPS):
        for index, offset in enumerate(offsets):
            chip = (z + offset * way + 2 * ring) % ring
            for half, which in enumerate((high, 1 - high)):
                send = pltpu.make_async_copy(terms.at[chip, which], target.at[index, half], out_sem.at[len(sends)])
                send.start()
                sends.append(send)

    place = owner_ref[...] * FRAME + slot_ref[...]
    chosen = (lax.broadcasted_iota(jnp.int32, (out.shape[0], x.shape[0]), 0) == place).astype(jnp.bfloat16)
    turned[...] = jnp.transpose(w[...])
    moved = jnp.dot(chosen, pair[...], preferred_element_type=jnp.float32).astype(jnp.bfloat16)
    parts = 2
    block = out.shape[0] // parts
    for part in range(parts):
        at = pl.ds(part * block, block)
        total = jnp.dot(moved[part * block : (part + 1) * block], turned[...], preferred_element_type=jnp.float32)
        out[at, :] = total.astype(jnp.bfloat16)
        send = pltpu.make_async_copy(out.at[at], out_hbm.at[at], out_sem.at[len(sends)])
        send.start()
        sends.append(send)
    for send in sends:
        send.wait()


def table_kernel(slots_ref, out_ref):
    tokens, frames = out_ref.shape
    slots = slots_ref.shape[1]
    capacity = slots * FRAME // frames
    held = (lax.broadcasted_iota(jnp.int32, (tokens, slots), 0) == slots_ref[...]).astype(jnp.bfloat16)
    place = lax.broadcasted_iota(jnp.int32, (slots, frames), 1)
    within = lax.bitwise_and(place, FRAME - 1)
    source = lax.shift_right_logical(place, FRAME.bit_length() - 1) * capacity + within
    spread = (lax.broadcasted_iota(jnp.int32, (slots, frames), 0) == source) & (within < capacity)
    out_ref[...] = jnp.dot(held, spread.astype(jnp.bfloat16), preferred_element_type=jnp.float32).astype(jnp.bfloat16)


def combine_kernel(table_ref, rows_ref, out_ref):
    out_ref[...] = jnp.dot(table_ref[...], rows_ref[...], preferred_element_type=jnp.float32).astype(jnp.bfloat16)


def adam_kernel(scale, parts, shard_ref, *refs):
    weights_ref, one_ref, two_ref, out_w, out_one, out_two = refs[parts:]
    total = refs[0][...].astype(jnp.float32)
    for ref in refs[1:parts]:
        total += ref[...].astype(jnp.float32)
    gradient = jnp.transpose(total) * scale
    new_one = BETA_ONE * one_ref[0] + (1.0 - BETA_ONE) * gradient
    new_two = BETA_TWO * two_ref[0] + (1.0 - BETA_TWO) * gradient * gradient
    update = new_one / CORR_ONE / (jnp.sqrt(new_two / CORR_TWO) + EPSILON)
    kept = weights_ref[0].astype(jnp.float32) * (1.0 - LEARN_RATE * WEIGHT_DECAY)
    out_w[0] = (kept - LEARN_RATE * update).astype(jnp.bfloat16)
    out_one[0] = new_one
    out_two[0] = new_two


def ring_sum(ahead, behind, far, up_own, down_own, up_next, down_next, own, wide, narrow):
    ring = narrow // 2

    def hop(value, steps, flip=0):
        pairs = []
        for w in range(wide):
            shift = steps * (1 - 2 * (w % 2))
            for n in range(narrow):
                to = ((n // 2 + shift) % ring) * 2 + (n % 2 + flip) % 2
                pairs.append((w * narrow + n, w * narrow + to))
        return lax.ppermute(value, ("wide", "narrow"), pairs)

    def add(*values):
        total = values[0].astype(jnp.float32)
        for value in values[1:]:
            total += value.astype(jnp.float32)
        return total.astype(jnp.bfloat16)

    ahead = hop(ahead, 1)
    behind = hop(behind, -1)
    far = hop(far, 2)
    up = hop(add(far[0], ahead[0], up_own[0]), 2)
    down = hop(add(behind[0], down_own[0]), -2)
    up = hop(add(up, ahead[1], up_next[0]), 2)
    down = hop(add(down, behind[1], down_next[0]), -2)
    across = hop(add(up[1], down[1], ahead[2, 1], behind[2, 1], own[0, 1]), 0, 1)
    return (ahead, behind, own, up[None], down[None]), (across,)


def step(weights, act_rows, grad_rows, row_owner, row_slot, slot_token, moment_one, moment_two):
    wide, narrow = lax.axis_size("wide"), lax.axis_size("narrow")
    rows, width = act_rows.shape[3:]
    units = weights.shape[2]
    shard_rows = moment_one.shape[1]
    tokens = 128
    grad_scale = 1.0 / math.sqrt(rows * narrow)
    x, dy, packed = act_rows[0, 0, 0], grad_rows[0, 0, 0], weights[0]
    anywhere, vmem, smem = (pl.BlockSpec(memory_space=m) for m in (pl.ANY, pltpu.VMEM, pltpu.SMEM))
    half = jnp.bfloat16
    shard = lax.axis_index("narrow").astype(jnp.int32).reshape(1)
    column = lax.axis_index("wide").astype(jnp.int32).reshape(1)

    sizes = [len(group) for group in GROUPS]
    *blocks, outgoing = pl.pallas_call(
        expert_kernel,
        out_shape=tuple(jax.ShapeDtypeStruct((n, 2, units, shard_rows), half) for n in sizes)
        + (jax.ShapeDtypeStruct((wide * FRAME, width), half),),
        in_specs=[smem] * 2 + [vmem] * 2 + [anywhere] * 3,
        out_specs=(anywhere,) * (len(sizes) + 1),
        scratch_shapes=[
            pltpu.VMEM((rows, width), half),
            pltpu.VMEM((rows, width), half),
            pltpu.VMEM((width, 2 * units), half),
            pltpu.VMEM((width, units), half),
            pltpu.VMEM((rows, 2 * units), half),
            pltpu.VMEM((rows, units), half),
            pltpu.VMEM((narrow // 2, 2, units, shard_rows), half),
            pltpu.VMEM((2 * units, width), half),
            pltpu.VMEM((wide * FRAME, width), half),
            pltpu.SemaphoreType.DMA((5,)),
            pltpu.SemaphoreType.DMA((2 * sum(sizes) + 2,)),
        ],
        cost_estimate=pl.CostEstimate(flops=7 * 10**9, bytes_accessed=12 * 10**6, transcendentals=3 * 10**5),
        name="expert",
    )(shard, column, row_owner[0], row_slot[0], x, dy, packed)
    stacks, parts = ring_sum(*blocks, wide, narrow)
    arrived = lax.all_to_all(
        outgoing.reshape(wide, FRAME, width), "wide", split_axis=0, concat_axis=0, tiled=True
    ).reshape(wide * FRAME, width)

    block = (1, shard_rows, units)
    whole = pl.BlockSpec(block, lambda i, s: (0, 0, 0))
    part = pl.BlockSpec((units, shard_rows), lambda i, s: (0, 0))
    stack = [pl.BlockSpec((None, None, units, shard_rows), lambda i, s, n=a.shape[0]: (n - 1, 0, 0, 0)) for a in stacks]
    new_weights, new_one, new_two = pl.pallas_call(
        lambda *refs: adam_kernel(grad_scale, len(stacks) + len(parts), *refs),
        out_shape=(
            jax.ShapeDtypeStruct(block, half),
            jax.ShapeDtypeStruct(block, jnp.float32),
            jax.ShapeDtypeStruct(block, jnp.float32),
        ),
        grid_spec=pltpu.PrefetchScalarGridSpec(
            num_scalar_prefetch=1,
            grid=(1,),
            in_specs=stack + [part] * len(parts) + [pl.BlockSpec(block, lambda i, s: (0, s[0], 0)), whole, whole],
            out_specs=(whole, whole, whole),
        ),
        compiler_params=pltpu.CompilerParams(vmem_limit_bytes=6 * 2**20),
        name="adam",
    )(shard, *stacks, *parts, weights, moment_one, moment_two)

    table = pl.pallas_call(
        table_kernel,
        out_shape=jax.ShapeDtypeStruct((tokens, wide * FRAME), half),
        in_specs=[vmem],
        out_specs=vmem,
        compiler_params=pltpu.CompilerParams(vmem_limit_bytes=16 * 2**20),
        cost_estimate=pl.CostEstimate(flops=4 * 10**9, bytes_accessed=3 * 10**5, transcendentals=0),
        name="table",
    )(slot_token[0])
    combined = pl.pallas_call(
        combine_kernel,
        out_shape=jax.ShapeDtypeStruct((tokens, width), half),
        in_specs=[vmem] * 2,
        out_specs=vmem,
        compiler_params=pltpu.CompilerParams(vmem_limit_bytes=16 * 2**20),
        cost_estimate=pl.CostEstimate(flops=3 * 10**8, bytes_accessed=3 * 10**6, transcendentals=0),
        name="combine",
    )(table, arrived)
    return (combined[None, None], new_weights, new_one, new_two)


def solution(mesh):
    in_specs = (
        P("wide", None, None),
        P("wide", "narrow", None, None, None),
        P("wide", "narrow", None, None, None),
        P("wide", "narrow", None),
        P("wide", "narrow", None),
        P("wide", "narrow", None),
        P("wide", "narrow", None),
        P("wide", "narrow", None),
    )
    out_specs = (
        P("wide", "narrow", None, None),
        P("wide", "narrow", None),
        P("wide", "narrow", None),
        P("wide", "narrow", None),
    )
    return jax.shard_map(step, mesh=mesh, in_specs=in_specs, out_specs=out_specs, check_vma=False)
```

```python
import math

import jax
import jax.numpy as jnp
from jax import lax
from jax.experimental import pallas as pl
from jax.experimental.pallas import tpu as pltpu
from jax.sharding import PartitionSpec as P

BETA_ONE = 0.9
BETA_TWO = 0.95
LEARN_RATE = 0.003
WEIGHT_DECAY = 0.1
EPSILON = 1e-08
CORR_ONE = 1.0 - 0.9**10
CORR_TWO = 1.0 - 0.95**10

FRAME = 32
LANES = 128

SENT, KEPT = ((5,), (-5,), (6,), (3, 1), (-3, -1)), (4, -4, 2, -2, 0)
GROUPS = (*SENT, *((offset,) for offset in KEPT))


def expert_kernel(narrow_ref, wide_ref, owner_ref, slot_ref, x_hbm, dy_hbm, w_hbm, *refs):
    targets, out_hbm = refs[: len(GROUPS)], refs[len(GROUPS)]
    x, dy, w, w_down, pair, hidden, terms, turned, out, in_sem, out_sem = refs[len(GROUPS) + 1 :]
    width, units = x.shape[1], hidden.shape[1]
    loads = [
        pltpu.make_async_copy(x_hbm, x, in_sem.at[0]),
        pltpu.make_async_copy(w_hbm.at[pl.ds(0, width)], w.at[:, pl.ds(0, units)], in_sem.at[1]),
        pltpu.make_async_copy(w_hbm.at[pl.ds(width, width)], w.at[:, pl.ds(units, units)], in_sem.at[2]),
        pltpu.make_async_copy(dy_hbm, dy, in_sem.at[3]),
        pltpu.make_async_copy(w_hbm.at[pl.ds(2 * width, width)], w_down, in_sem.at[4]),
    ]
    for load in loads:
        load.start()
    for load in loads[:3]:
        load.wait()
    rows = x.shape[0]
    cut = -(-rows // 32) * 16
    blocks = (slice(0, cut), slice(cut, rows))
    products = [jnp.dot(x[at, :], w[...], preferred_element_type=jnp.float32) for at in blocks]
    for load in loads[3:]:
        load.wait()
    for at, both in zip(blocks, products):
        gate, up = both[:, :units], both[:, units:]
        d_hidden = jnp.dot(dy[at, :], w_down[...], preferred_element_type=jnp.float32)
        prob = jax.nn.sigmoid(gate)
        active = gate * prob
        hidden[at, :] = (active * up).astype(jnp.bfloat16)
        pair[at, units:] = (d_hidden * active).astype(jnp.bfloat16)
        pair[at, :units] = (d_hidden * up * prob * (1.0 + gate * (1.0 - prob))).astype(jnp.bfloat16)
    sends = []

    ring = terms.shape[0]
    per = width // LANES
    first = (((0,), (0,)), ((), ()))
    for start, left, right in ((0, pair, x), (2 * per, hidden, dy)):
        product = lax.dot_general(left[...], right[...], first, preferred_element_type=jnp.float32)
        product = product.astype(jnp.bfloat16)
        for at in range(start, start + per * left.shape[1] // units):
            row, block = (at - start) // per * units, at % per * LANES
            terms[at // 2, at % 2] = product[row : row + units, block : block + LANES]

    z, high = narrow_ref[0] // 2, narrow_ref[0] % 2
    way = 1 - 2 * (wide_ref[0] % 2)
    for target, offsets in zip(targets, GROUPS):
        for index, offset in enumerate(offsets):
            chip = (z + offset * way + 2 * ring) % ring
            for half, which in enumerate((high, 1 - high)):
                send = pltpu.make_async_copy(terms.at[chip, which], target.at[index, half], out_sem.at[len(sends)])
                send.start()
                sends.append(send)

    place = owner_ref[...] * FRAME + slot_ref[...]
    chosen = (lax.broadcasted_iota(jnp.int32, (out.shape[0], x.shape[0]), 0) == place).astype(jnp.bfloat16)
    turned[...] = jnp.transpose(w[...])
    moved = jnp.dot(chosen, pair[...], preferred_element_type=jnp.float32).astype(jnp.bfloat16)
    parts = 2
    block = out.shape[0] // parts
    for part in range(parts):
        at = pl.ds(part * block, block)
        total = jnp.dot(moved[part * block : (part + 1) * block], turned[...], preferred_element_type=jnp.float32)
        out[at, :] = total.astype(jnp.bfloat16)
        send = pltpu.make_async_copy(out.at[at], out_hbm.at[at], out_sem.at[len(sends)])
        send.start()
        sends.append(send)
    for send in sends:
        send.wait()


def table_kernel(slots_ref, out_ref):
    tokens, frames = out_ref.shape
    slots = slots_ref.shape[1]
    capacity = slots * FRAME // frames
    held = (lax.broadcasted_iota(jnp.int32, (tokens, slots), 0) == slots_ref[...]).astype(jnp.bfloat16)
    place = lax.broadcasted_iota(jnp.int32, (slots, frames), 1)
    within = lax.bitwise_and(place, FRAME - 1)
    source = lax.shift_right_logical(place, FRAME.bit_length() - 1) * capacity + within
    spread = (lax.broadcasted_iota(jnp.int32, (slots, frames), 0) == source) & (within < capacity)
    out_ref[...] = jnp.dot(held, spread.astype(jnp.bfloat16), preferred_element_type=jnp.float32).astype(jnp.bfloat16)


def combine_kernel(table_ref, rows_ref, out_ref):
    out_ref[...] = jnp.dot(table_ref[...], rows_ref[...], preferred_element_type=jnp.float32).astype(jnp.bfloat16)


def adam_kernel(scale, parts, shard_ref, *refs):
    weights_ref, one_ref, two_ref, out_w, out_one, out_two = refs[parts:]
    total = refs[0][...].astype(jnp.float32)
    for ref in refs[1:parts]:
        total += ref[...].astype(jnp.float32)
    gradient = jnp.transpose(total) * scale
    new_one = BETA_ONE * one_ref[0] + (1.0 - BETA_ONE) * gradient
    new_two = BETA_TWO * two_ref[0] + (1.0 - BETA_TWO) * gradient * gradient
    update = new_one / CORR_ONE / (jnp.sqrt(new_two / CORR_TWO) + EPSILON)
    kept = weights_ref[0].astype(jnp.float32) * (1.0 - LEARN_RATE * WEIGHT_DECAY)
    out_w[0] = (kept - LEARN_RATE * update).astype(jnp.bfloat16)
    out_one[0] = new_one
    out_two[0] = new_two


def ring_sum(
    ahead, behind, far, ahead_late, behind_late, up_own, down_own, up_next, down_next, own, wide, narrow
):
    ring = narrow // 2

    def hop(value, steps, flip=0):
        pairs = []
        for w in range(wide):
            shift = steps * (1 - 2 * (w % 2))
            for n in range(narrow):
                to = ((n // 2 + shift) % ring) * 2 + (n % 2 + flip) % 2
                pairs.append((w * narrow + n, w * narrow + to))
        return lax.ppermute(value, ("wide", "narrow"), pairs)

    def add(*values):
        total = values[0].astype(jnp.float32)
        for value in values[1:]:
            total += value.astype(jnp.float32)
        return total.astype(jnp.bfloat16)

    ahead = hop(ahead, 1)
    behind = hop(behind, -1)
    far = hop(far, 2)
    ahead_late = hop(ahead_late, 1)
    behind_late = hop(behind_late, -1)
    up = hop(add(far[0], ahead[0], up_own[0]), 2)
    down = hop(add(behind[0], down_own[0]), -2)
    up = hop(add(up, ahead_late[0], up_next[0]), 2)
    down = hop(add(down, behind_late[0], down_next[0]), -2)
    across = hop(add(up[1], down[1], ahead_late[1, 1], behind_late[1, 1], own[0, 1]), 0, 1)
    return (ahead_late, behind_late, own, up[None], down[None]), (across,)


def step(weights, act_rows, grad_rows, row_owner, row_slot, slot_token, moment_one, moment_two):
    wide, narrow = lax.axis_size("wide"), lax.axis_size("narrow")
    rows, width = act_rows.shape[3:]
    units = weights.shape[2]
    shard_rows = moment_one.shape[1]
    tokens = 128
    grad_scale = 1.0 / math.sqrt(rows * narrow)
    x, dy, packed = act_rows[0, 0, 0], grad_rows[0, 0, 0], weights[0]
    anywhere, vmem, smem = (pl.BlockSpec(memory_space=m) for m in (pl.ANY, pltpu.VMEM, pltpu.SMEM))
    half = jnp.bfloat16
    shard = lax.axis_index("narrow").astype(jnp.int32).reshape(1)
    column = lax.axis_index("wide").astype(jnp.int32).reshape(1)

    sizes = [len(group) for group in GROUPS]
    *blocks, outgoing = pl.pallas_call(
        expert_kernel,
        out_shape=tuple(jax.ShapeDtypeStruct((n, 2, units, shard_rows), half) for n in sizes)
        + (jax.ShapeDtypeStruct((wide * FRAME, width), half),),
        in_specs=[smem] * 2 + [vmem] * 2 + [anywhere] * 3,
        out_specs=(anywhere,) * (len(sizes) + 1),
        scratch_shapes=[
            pltpu.VMEM((rows, width), half),
            pltpu.VMEM((rows, width), half),
            pltpu.VMEM((width, 2 * units), half),
            pltpu.VMEM((width, units), half),
            pltpu.VMEM((rows, 2 * units), half),
            pltpu.VMEM((rows, units), half),
            pltpu.VMEM((narrow // 2, 2, units, shard_rows), half),
            pltpu.VMEM((2 * units, width), half),
            pltpu.VMEM((wide * FRAME, width), half),
            pltpu.SemaphoreType.DMA((5,)),
            pltpu.SemaphoreType.DMA((2 * sum(sizes) + 2,)),
        ],
        cost_estimate=pl.CostEstimate(flops=7 * 10**9, bytes_accessed=12 * 10**6, transcendentals=3 * 10**5),
        name="expert",
    )(shard, column, row_owner[0], row_slot[0], x, dy, packed)
    stacks, parts = ring_sum(*blocks, wide, narrow)
    arrived = lax.all_to_all(
        outgoing.reshape(wide, FRAME, width), "wide", split_axis=0, concat_axis=0, tiled=True
    ).reshape(wide * FRAME, width)

    block = (1, shard_rows, units)
    whole = pl.BlockSpec(block, lambda i, s: (0, 0, 0))
    part = pl.BlockSpec((units, shard_rows), lambda i, s: (0, 0))
    stack = [pl.BlockSpec((None, None, units, shard_rows), lambda i, s, n=a.shape[0]: (n - 1, 0, 0, 0)) for a in stacks]
    new_weights, new_one, new_two = pl.pallas_call(
        lambda *refs: adam_kernel(grad_scale, len(stacks) + len(parts), *refs),
        out_shape=(
            jax.ShapeDtypeStruct(block, half),
            jax.ShapeDtypeStruct(block, jnp.float32),
            jax.ShapeDtypeStruct(block, jnp.float32),
        ),
        grid_spec=pltpu.PrefetchScalarGridSpec(
            num_scalar_prefetch=1,
            grid=(1,),
            in_specs=stack + [part] * len(parts) + [pl.BlockSpec(block, lambda i, s: (0, s[0], 0)), whole, whole],
            out_specs=(whole, whole, whole),
        ),
        compiler_params=pltpu.CompilerParams(vmem_limit_bytes=6 * 2**20),
        name="adam",
    )(shard, *stacks, *parts, weights, moment_one, moment_two)

    table = pl.pallas_call(
        table_kernel,
        out_shape=jax.ShapeDtypeStruct((tokens, wide * FRAME), half),
        in_specs=[vmem],
        out_specs=vmem,
        compiler_params=pltpu.CompilerParams(vmem_limit_bytes=16 * 2**20),
        cost_estimate=pl.CostEstimate(flops=4 * 10**9, bytes_accessed=3 * 10**5, transcendentals=0),
        name="table",
    )(slot_token[0])
    combined = pl.pallas_call(
        combine_kernel,
        out_shape=jax.ShapeDtypeStruct((tokens, width), half),
        in_specs=[vmem] * 2,
        out_specs=vmem,
        compiler_params=pltpu.CompilerParams(vmem_limit_bytes=16 * 2**20),
        cost_estimate=pl.CostEstimate(flops=3 * 10**8, bytes_accessed=3 * 10**6, transcendentals=0),
        name="combine",
    )(table, arrived)
    return (combined[None, None], new_weights, new_one, new_two)


def solution(mesh):
    in_specs = (
        P("wide", None, None),
        P("wide", "narrow", None, None, None),
        P("wide", "narrow", None, None, None),
        P("wide", "narrow", None),
        P("wide", "narrow", None),
        P("wide", "narrow", None),
        P("wide", "narrow", None),
        P("wide", "narrow", None),
    )
    out_specs = (
        P("wide", "narrow", None, None),
        P("wide", "narrow", None),
        P("wide", "narrow", None),
        P("wide", "narrow", None),
    )
    return jax.shard_map(step, mesh=mesh, in_specs=in_specs, out_specs=out_specs, check_vma=False)
```
